32 devices in a mesh: wide: 16 (over z, y, core), shift: 2 (over x).
Axes of the slice: x: 2, y: 2, z: 4, core: 2. Of those that a mesh axis runs over, the one named last changes fastest.
Arguments:
- particles: bfloat16 [1024, 8448], P('wide'), may hold values from -64 to 64
- group_id: int32 [1024, 1], P('wide'), may hold values from 0 to 15; in each aligned block of 64 rows (0 to 63, 64 to 127, ...) at most 8 rows name the same one
- ctf_curves: float32 [16, 4224], P('wide'), may hold values from -1 to 1
- projections: bfloat16 [16, 8448], P('wide')
- inv_noise: float32 [4224], replicated, may hold values from 0.5 to 2
- shifts: int32 [64, 2], P('shift'), may hold values from -8 to 8
Outputs:
- insertion: float32 [16, 12672], P('wide')
- log_evidence: float32 [1024], P('wide')
The draws below stay inside these ranges and needn't reach their ends.
Inputs may be any that keep to these rules, and one draw needn't show every extreme that they name: `group_id`: at most 8 of the rows of one device name the same group, a bound that some block reaches.
All inputs are finite; a program needn't handle non-finite values.
Results may differ from the reference program's by a relative error of at most 0.0029.
Values may be sent and summed in bfloat16 or wider, within the bound.
A program may use at most 64 MiB of HBM per device.

```python
import math
import jax
import jax.numpy as jnp
import numpy as np
from jax import lax

COEFFS = 4224
NTRANS = 64
PART_DEV = 64
PARTICLES = 1024
GROUPS = 16
ORIENT = 16
CAPACITY = 8


def base_values(value_key, row_count, col_count):
    values = jnp.clip(jax.random.normal(value_key, (row_count, col_count), jnp.float32), -3.0, 3.0)
    return values


def draw_particles(key, part):
    base_key = jax.random.fold_in(key, 101)
    scale_key, value_key = jax.random.split(base_key, 2)
    row_scale = jnp.exp(jax.random.uniform(scale_key, (PARTICLES, 1), jnp.float32, math.log(0.1), math.log(1.0)))
    values = row_scale * base_values(value_key, PARTICLES, 2 * COEFFS)
    return values.astype(jnp.bfloat16)


def draw_projections(key, part):
    base_key = jax.random.fold_in(key, 202)
    value_key = jax.random.fold_in(base_key, 0)
    factor = 2.6 / math.sqrt(2.0 * COEFFS)
    values = base_values(value_key, ORIENT, 2 * COEFFS) * factor
    return values.astype(jnp.bfloat16)


def draw_inv_noise(key, part):
    noise_key = jax.random.fold_in(key, 303)
    return jnp.exp(jax.random.uniform(noise_key, (COEFFS,), jnp.float32, math.log(0.5), math.log(2.0)))


def touch_ends(values, own_key, low, top_value):
    spot = [jax.random.randint(jax.random.fold_in(own_key, axis), (), 0, length) for axis, length in enumerate(values.shape)]
    main_axis = values.shape.index(max(values.shape))
    neighbour = spot[:main_axis] + [(spot[main_axis] + 1) % values.shape[main_axis]] + spot[main_axis + 1:]
    return values.at[tuple(spot)].set(low).at[tuple(neighbour)].set(top_value)


def shard_levels(own_key, shape, cuts, low, high):
    factor_of, own = 1.0, jax.random.fold_in(own_key, 6)
    for dim, parts in cuts:
        draws = jnp.exp(jax.random.uniform(jax.random.fold_in(own, dim), (parts,), jnp.float32, low / len(cuts), high / len(cuts)))
        factor_of = factor_of * jnp.repeat(draws, shape[dim] // parts).reshape([-1 if axis == dim else 1 for axis in range(len(shape))])
    return factor_of


def shared_out(own_key, own, number, rows, number_of, top, reach, slope):
    ranking = jax.random.permutation(own_key, number_of)
    heavy_load, usual = portions_of(number_of, rows * top, reach, slope, True), portions_of(number_of, rows * top, reach, slope, False)
    places = jnp.arange(number_of)

    def named(lengths, offset_by):
        used = int((lengths > 0).sum())
        fixed = max(1, used // 4)
        shifted = fixed + (places - fixed + offset_by * (used - fixed)) % max(1, number_of - fixed)
        return jnp.zeros((number_of,), jnp.int32).at[ranking[jnp.where(places < fixed, places, shifted)]].set(jnp.asarray(lengths, jnp.int32))

    lengths = jnp.where(number % 4 == 0, named(heavy_load, number // 4), named(usual, number - number // 4 - 1))
    mixed = jax.random.permutation(jax.random.fold_in(own, 3), number_of)
    donor, receiver = mixed[0:number_of // 2 * 2:2], mixed[1:number_of // 2 * 2:2]
    margin = jnp.minimum(lengths[donor] - 1, reach - lengths[receiver]) // 2
    margin = jnp.where((donor == ranking[0]) | (receiver == ranking[0]) | (lengths[receiver] == 0), 0, jnp.maximum(margin, 0))
    shifted = jax.random.randint(jax.random.fold_in(own, 4), (number_of // 2,), 0, 1 << 20) % (margin + 1)
    lengths = lengths.at[donor].add(-shifted).at[receiver].add(shifted)
    members = jnp.searchsorted(jnp.cumsum(lengths), jnp.arange(rows * top), side="right").astype(jnp.int32)
    table = members.reshape(top, rows).T
    table = table[jax.random.permutation(jax.random.fold_in(own, 1), rows)]
    offset_by = jax.random.randint(jax.random.fold_in(own, 2), (rows, 1), 0, top)
    return jnp.take_along_axis(table, (jnp.arange(top)[None, :] + offset_by) % top, axis=1)


def portions_of(number_of, total, most, slope, full):
    portions = [(1 << 20) // math.isqrt(rank ** slope) + 1 for rank in range(1, number_of + 1)]
    largest = most if full else min(most, max(-(-total // number_of), total * portions[0] // sum(portions)))
    least = 1 if total - largest >= number_of - 1 else 0
    counts, surplus = [largest] + [least] * (number_of - 1), total - largest - least * (number_of - 1)
    while surplus > 0:
        movable = [i for i in range(1, number_of) if counts[i] < largest] or [i for i in range(1, number_of) if counts[i] < most]
        pool, left = sum([portions[i] for i in movable]), surplus
        for i in movable:
            addition = min(most - counts[i], max(1, left * portions[i] // pool), surplus)
            counts[i] = counts[i] + addition
            surplus = surplus - addition
    return np.array(counts)


def setup_inputs(seed: int = 0) -> dict:
    arg_keys = jax.random.split(jax.random.key(seed), 7)
    particles = draw_particles(jax.random.fold_in(arg_keys[6], 71), 0)
    group_id_keys = jax.random.split(jax.random.fold_in(arg_keys[1], 1), PARTICLES // PART_DEV)
    group_id_turns = jax.random.permutation(jax.random.fold_in(arg_keys[1], 3), PARTICLES // PART_DEV)
    group_id = jax.vmap(lambda own, number: shared_out(jax.random.fold_in(arg_keys[1], 2), own, number, PART_DEV, GROUPS, 1, CAPACITY, 2))(group_id_keys, group_id_turns).reshape((PARTICLES, 1))
    ctf_curves = jnp.clip(jax.random.uniform(arg_keys[2], (GROUPS, COEFFS), jnp.float32, -1.0, 1.0) * shard_levels(arg_keys[2], (GROUPS, COEFFS), ((0, 16),), -0.4, 0.0), -1.0, 1.0)
    projections = draw_projections(jax.random.fold_in(arg_keys[6], 71), 0)
    inv_noise = draw_inv_noise(jax.random.fold_in(arg_keys[6], 71), 0)
    shifts = touch_ends(jax.random.randint(arg_keys[5], (NTRANS, 2), -8, 9), jax.random.fold_in(arg_keys[5], 1), -8, 8).astype(jnp.int32)
    return {"particles": particles, "group_id": group_id, "ctf_curves": ctf_curves, "projections": projections, "inv_noise": inv_noise, "shifts": shifts}


TWO_PI_BOX = 2.0 * math.pi / 128.0


def shift_tables(shifts, coeffs):
    coeff_index = jnp.arange(coeffs, dtype=jnp.int32)
    freq_x = (coeff_index // 128).astype(jnp.float32)
    freq_y = (coeff_index % 128 - 64).astype(jnp.float32)
    move_x = shifts[:, 0].astype(jnp.float32)
    move_y = shifts[:, 1].astype(jnp.float32)
    phase_angle = TWO_PI_BOX * (move_x[:, None] * freq_x[None, :] + move_y[:, None] * freq_y[None, :])
    return jnp.cos(phase_angle), jnp.sin(phase_angle)


def rotate_slices(slab, cos_table, sin_table):
    coeffs = cos_table.shape[1]
    real_part = slab[:, :coeffs].astype(jnp.float32)[:, None, :]
    imag_part = slab[:, coeffs:].astype(jnp.float32)[:, None, :]
    rot_real = real_part * cos_table[None] + imag_part * sin_table[None]
    rot_imag = imag_part * cos_table[None] - real_part * sin_table[None]
    joined = jnp.concatenate([rot_real, rot_imag], 2)
    return joined.reshape(slab.shape[0] * cos_table.shape[0], 2 * coeffs).astype(jnp.bfloat16)


def reference(particles, group_id, ctf_curves, projections, inv_noise, shifts):
    groups = group_id[:, 0].astype(jnp.int32)
    ctf_row = ctf_curves[groups]
    real_part = particles[:, :COEFFS].astype(jnp.float32)
    imag_part = particles[:, COEFFS:].astype(jnp.float32)
    noise_ctf = inv_noise[None, :] * ctf_row
    weighted = jnp.concatenate([noise_ctf * real_part, noise_ctf * imag_part], 1).astype(jnp.bfloat16)
    filtered = jnp.concatenate([ctf_row * real_part, ctf_row * imag_part], 1).astype(jnp.bfloat16)
    cos_table, sin_table = shift_tables(shifts, COEFFS)
    rotated = rotate_slices(projections, cos_table, sin_table)
    cross_term = jnp.dot(weighted, rotated.T, preferred_element_type=jnp.float32)
    slice_real = projections[:, :COEFFS].astype(jnp.float32)
    slice_imag = projections[:, COEFFS:].astype(jnp.float32)
    slice_power = slice_real * slice_real + slice_imag * slice_imag
    weight_sq = ctf_row * ctf_row * inv_noise[None, :]
    self_term = 0.5 * jnp.dot(weight_sq, slice_power.T, precision=lax.Precision.HIGHEST)
    scores = cross_term.reshape(PARTICLES, ORIENT, NTRANS) - self_term[:, :, None]
    row_max = jnp.max(scores, axis=(1, 2))
    exp_scores = jnp.exp(scores - row_max[:, None, None])
    row_total = jnp.sum(exp_scores, axis=(1, 2))
    weights = (exp_scores / row_total[:, None, None]).astype(jnp.bfloat16)
    log_evidence = row_max + jnp.log(row_total)
    flat_weights = weights.reshape(PARTICLES, ORIENT * NTRANS)
    update = jnp.dot(flat_weights.T, filtered, preferred_element_type=jnp.float32)
    update = update.reshape(ORIENT, NTRANS, 2 * COEFFS)
    upd_real = update[:, :, :COEFFS]
    upd_imag = update[:, :, COEFFS:]
    data_real = jnp.sum(upd_real * cos_table[None] - upd_imag * sin_table[None], 1)
    data_imag = jnp.sum(upd_real * sin_table[None] + upd_imag * cos_table[None], 1)
    weight_sum = jnp.sum(weights.astype(jnp.float32), 2)
    weight_data = jnp.dot(weight_sum.T, ctf_row * ctf_row, precision=lax.Precision.HIGHEST)
    insertion = jnp.concatenate([data_real, data_imag, weight_data], 1)
    return insertion, log_evidence
```

```python
import functools
import math

import jax
import jax.numpy as jnp
from jax import lax
from jax.experimental import pallas as pl
from jax.experimental.pallas import tpu as pltpu
from jax.sharding import PartitionSpec as P

LANE = 128
STEP = 2.0 * math.pi / 128.0
HIGH = lax.Precision.HIGHEST
MESH = pl.DeviceIdType.MESH
F32 = jnp.float32
BF16 = jnp.bfloat16
NT_DIMS = (((1,), (1,)), ((), ()))
NN_DIMS = (((1,), (0,)), ((), ()))


def dot(a, b, dims=NN_DIMS, precision=None):
    return lax.dot_general(a, b, dims, precision=precision, preferred_element_type=F32)


def kernel(
    cfg, x_hbm, gid_ref, ctf_ref, proj_ref, noise_ref, sh_ref,
    out_ref, ev_ref,
    xbuf, cbuf, pbuf, shbuf, cos_t, sin_t, wgt, fil, wsq, pf, power, selfc,
    sc, scr, tot, wts, wsum, part, r1, r2, fin, fbuf,
    x_sem, own_sem, ag_ssem, ag_rsem, rl_ssem, sh_ssem, sh_rsem,
    sc_ssem, sc_rsem, r1_ssem, r1_rsem, r2_ssem, r2_rsem, f_ssem, f_rsem,
):
    W, S, nl, L, NTL, R = cfg
    C = L * LANE
    NT = NTL * S
    H = W // 2
    NC = W // 2
    QB = 2
    NB = H // QB
    RB = QB * NT
    w = lax.axis_index("wide")
    s = lax.axis_index("shift")
    core = lax.rem(w, 2)
    chip = lax.div(w, 2)
    mate = chip * 2 + (1 - core)
    first = jnp.minimum(s * L, nl - L)
    start = pl.multiple_of(first * LANE, LANE)
    full = nl * LANE
    window = pl.ds(start, C)

    def chip_at(k):
        return lax.rem(chip + k, NC)

    def remote(src, dst, ssem, rsem, wide=None, shift=None):
        return pltpu.make_async_remote_copy(
            src_ref=src, dst_ref=dst, send_sem=ssem, recv_sem=rsem,
            device_id=(w if wide is None else wide, s if shift is None else shift),
            device_id_type=MESH,
        )

    x_copies = [
        pltpu.make_async_copy(
            x_hbm.at[:, pl.ds(pl.multiple_of(start + h * full, LANE), C)],
            xbuf.at[h], x_sem.at[h],
        )
        for h in range(2)
    ]
    own = [
        pltpu.make_async_copy(ctf_ref.at[:, window], cbuf.at[w], own_sem.at[0]),
        pltpu.make_async_copy(proj_ref.at[:, window], pbuf.at[w], own_sem.at[1]),
        pltpu.make_async_copy(sh_ref, shbuf.at[s], own_sem.at[2]),
    ]
    for c in own + x_copies:
        c.start()

    bar = pltpu.get_barrier_semaphore()
    pl.semaphore_signal(bar, inc=1, device_id=(mate, s), device_id_type=MESH)

    def greet(k, carry):
        pl.semaphore_signal(
            bar, inc=1, device_id=(chip_at(k) * 2 + core, s), device_id_type=MESH
        )
        return carry

    lax.fori_loop(1, NC, greet, 0)
    for d in range(1, S):
        pl.semaphore_signal(
            bar, inc=1, device_id=(w, lax.rem(s + d, S)), device_id_type=MESH
        )
    pl.semaphore_wait(bar, NC + S - 1)

    def ag_pair(k, to):
        return (
            remote(ctf_ref.at[:, window], cbuf.at[w], ag_ssem.at[0, k], ag_rsem.at[0, w], wide=to),
            remote(proj_ref.at[:, window], pbuf.at[w], ag_ssem.at[1, k], ag_rsem.at[1, w], wide=to),
        )

    def relay_pair(src):
        return (
            remote(cbuf.at[src], cbuf.at[src], rl_ssem.at[0, src], ag_rsem.at[0, src], wide=mate),
            remote(pbuf.at[src], pbuf.at[src], rl_ssem.at[1, src], ag_rsem.at[1, src], wide=mate),
        )

    sh_copies = [
        remote(sh_ref, shbuf.at[s], sh_ssem.at[d - 1], sh_rsem.at[s], shift=lax.rem(s + d, S))
        for d in range(1, S)
    ]
    for c in sh_copies:
        c.start()

    def ag_start(k, carry):
        for c in ag_pair(k, chip_at(k) * 2 + core):
            c.start()
        return carry

    lax.fori_loop(1, NC, ag_start, 0)
    for c in ag_pair(0, mate):
        c.start()

    for c in own:
        c.wait()
    for d in range(1, S):
        other = lax.rem(s + d, S)
        remote(sh_ref, shbuf.at[other], sh_ssem.at[d - 1], sh_rsem.at[other], shift=other).wait_recv()

    sh = shbuf[...].reshape(NT, LANE)
    lane = lax.broadcasted_iota(jnp.int32, (NT, LANE), 1)
    ang_b = STEP * (sh[:, 1:2] * (lane - 64).astype(F32))
    kx = first + lane
    ang_a = STEP * (sh[:, 0:1] * kx.astype(F32))
    live = jnp.where(kx >= s * L, 1.0, 0.0)
    cos_b, sin_b = jnp.cos(ang_b), jnp.sin(ang_b)
    cos_a, sin_a = jnp.cos(ang_a) * live, jnp.sin(ang_a) * live
    for l in range(L):
        ca, sa = cos_a[:, l : l + 1], sin_a[:, l : l + 1]
        cols = pl.ds(l * LANE, LANE)
        cos_t[:, cols] = ca * cos_b - sa * sin_b
        sin_t[:, cols] = sa * cos_b + ca * sin_b

    def relay(k, carry):
        src = lax.rem(chip + NC - k, NC) * 2 + core
        for c in relay_pair(src):
            c.wait_recv()
            c.start()
        return carry

    lax.fori_loop(1, NC, relay, 0)

    def landed(j, carry):
        for c in relay_pair(j * 2 + (1 - core)):
            c.wait_recv()
        return carry

    lax.fori_loop(0, NC, landed, 0)
    for c in x_copies:
        c.wait()

    onehot = jnp.where(
        gid_ref[...] == lax.broadcasted_iota(jnp.int32, (R, part.shape[2] - C), 1), 1.0, 0.0
    )
    pick = onehot[:, :W]
    for l in range(L):
        cols = pl.ds(l * LANE, LANE)
        curves = cbuf[:, 0, cols]
        row = dot(pick, curves, precision=HIGH)
        noise = noise_ref[:, pl.ds(pl.multiple_of(start + l * LANE, LANE), LANE)]
        x_re = xbuf[0, :, cols].astype(F32)
        x_im = xbuf[1, :, cols].astype(F32)
        gain = noise * row
        re, im = pl.ds(2 * l * LANE, LANE), pl.ds((2 * l + 1) * LANE, LANE)
        wgt[:, re] = (gain * x_re).astype(BF16)
        wgt[:, im] = (gain * x_im).astype(BF16)
        fil[:, re] = (row * x_re).astype(BF16)
        fil[:, im] = (row * x_im).astype(BF16)
        here = jnp.where(first + l >= s * L, 0.5, 0.0)
        wsq[:, cols] = curves * curves * noise * here

    def widen(o, carry):
        p = pbuf[o].astype(F32)
        pf[o] = p
        power[pl.ds(o, 1), :] = jnp.sum(p * p, axis=0, keepdims=True)
        return carry

    lax.fori_loop(0, W, widen, 0)
    self_g = dot(power[...], wsq[...], NT_DIMS, HIGH)
    self_i = dot(self_g, pick, NT_DIMS, HIGH)
    selfc[...] = jnp.concatenate([self_i[:H], self_i[H:]], axis=1)

    def sc_copy(b, d):
        rows = pl.ds(pl.multiple_of(b * RB, RB), RB)
        return remote(
            sc.at[rows], scr.at[d - 1, rows], sc_ssem.at[d - 1, b], sc_rsem.at[d - 1, b],
            shift=lax.rem(s + d, S),
        )

    def score_block(b, carry):
        acc = jnp.zeros((2 * RB, R), F32)
        for l in range(L):
            cols = pl.ds(l * LANE, LANE)
            ct, st = cos_t[:, cols], sin_t[:, cols]
            rots = []
            for h in range(2):
                for q in range(QB):
                    o = h * H + b * QB + q
                    pr = pf[o, 0:1, cols]
                    pi = pf[o, 1:2, cols]
                    rots.append(
                        jnp.concatenate(
                            [(pr * ct + pi * st).astype(BF16), (pi * ct - pr * st).astype(BF16)],
                            axis=1,
                        )
                    )
            rot = jnp.concatenate(rots, axis=0)
            acc = acc + dot(rot, wgt[:, pl.ds(2 * l * LANE, 2 * LANE)], NT_DIMS)
        both = jnp.concatenate([acc[:RB], acc[RB:]], axis=1)
        for q in range(QB):
            rows = pl.ds(pl.multiple_of(b * RB + q * NT, NT), NT)
            sc[rows, :] = both[q * NT : (q + 1) * NT] - selfc[pl.ds(b * QB + q, 1), :]
        for d in range(1, S):
            sc_copy(b, d).start()
        return carry

    lax.fori_loop(0, NB, score_block, 0)

    def swap(v):
        return pltpu.roll(v, R, 1)

    def join(b, m):
        rows = pl.ds(pl.multiple_of(b * RB, RB), RB)
        v = sc[rows, :]
        for d in range(1, S):
            sc_copy(b, d).wait_recv()
            v = v + scr[d - 1, rows, :]
        tot[rows, :] = v
        return jnp.maximum(m, jnp.max(v.reshape(RB // 8, 8, 2 * R), axis=0))

    m8 = lax.fori_loop(0, NB, join, jnp.full((8, 2 * R), -jnp.inf, F32))
    top = jnp.max(m8, axis=0, keepdims=True)
    top = jnp.maximum(top, swap(top))

    def expo(b, t):
        rows = pl.ds(pl.multiple_of(b * RB, RB), RB)
        e = jnp.exp(tot[rows, :] - top)
        tot[rows, :] = e
        return t + jnp.sum(e.reshape(RB // 8, 8, 2 * R), axis=0)

    t8 = lax.fori_loop(0, NB, expo, jnp.zeros((8, 2 * R), F32))
    total = jnp.sum(t8, axis=0, keepdims=True)
    total = total + swap(total)
    ev_ref[...] = (top + jnp.log(total))[:, :R]

    def norm(o, carry):
        rows = pl.ds(pl.multiple_of(o * NT, NT), NT)
        v = (tot[rows, :] / total).astype(BF16)
        wts[0, rows, :] = v[:, :R]
        wts[1, rows, :] = v[:, R:]
        wsum[pl.ds(o, 1), :] = jnp.sum(v.astype(F32), axis=0, keepdims=True)
        return carry

    lax.fori_loop(0, H, norm, 0)

    loads = wsum[...]
    extra = pl.ds(C, part.shape[2] - C)
    for h in range(2):
        load = dot(loads[:, h * R : (h + 1) * R], onehot, precision=HIGH)
        for o in range(H):
            part[h * H + o, 0:1, extra] = load[o : o + 1]
            part[h * H + o, 1:2, extra] = jnp.zeros_like(load[o : o + 1])

    def update_line(l, carry):
        cols = pl.ds(pl.multiple_of(l * LANE, LANE), LANE)
        ct, st = cos_t[:, cols], sin_t[:, cols]
        data = fil[:, pl.ds(pl.multiple_of(l * 2 * LANE, LANE), 2 * LANE)]
        for h in range(2):
            for o in range(0, H, 4):
                u = dot(wts[h, o * NT : (o + 4) * NT, :], data)
                for q in range(4):
                    ur = u[q * NT : (q + 1) * NT, :LANE]
                    ui = u[q * NT : (q + 1) * NT, LANE:]
                    at = h * H + o + q
                    part[at, 0:1, cols] = jnp.sum(ur * ct - ui * st, axis=0, keepdims=True)
                    part[at, 1:2, cols] = jnp.sum(ur * st + ui * ct, axis=0, keepdims=True)
        return carry

    lax.fori_loop(0, L, update_line, 0)

    def r1_copy(j):
        return remote(part.at[2 * j + (1 - core)], r1.at[j], r1_ssem.at[j], r1_rsem.at[j], wide=mate)

    def r2_copy(k):
        to = chip_at(k)
        return remote(
            part.at[2 * to + core], r2.at[k], r2_ssem.at[k], r2_rsem.at[k], wide=2 * to + core
        )

    def r1_start(k, carry):
        r1_copy(chip_at(k)).start()
        return carry

    lax.fori_loop(1, NC, r1_start, 0)
    r1_copy(chip).start()

    def r1_take(k, carry):
        j = chip_at(k)
        r1_copy(j).wait_recv()
        part[2 * j + core] = part[2 * j + core] + r1[j]
        r2_copy(k).start()
        return carry

    lax.fori_loop(1, NC, r1_take, 0)
    r1_copy(chip).wait_recv()
    fin[...] = part[w] + r1[chip]

    def r2_take(k, carry):
        r2_copy(k).wait_recv()
        fin[...] = fin[...] + r2[k]
        return carry

    lax.fori_loop(1, NC, r2_take, 0)

    load = fin[0:1, C : C + W]
    curves = cbuf[:, 0, :]
    fbuf[s, 0:2, :] = fin[:, :C]
    fbuf[s, 2:3, :] = dot(load, curves * curves, precision=HIGH)

    def f_copy(d):
        return remote(
            fbuf.at[s], fbuf.at[s], f_ssem.at[d - 1], f_rsem.at[s], shift=lax.rem(s + d, S)
        )

    for d in range(1, S):
        f_copy(d).start()
    for d in range(1, S):
        other = lax.rem(s + d, S)
        remote(fbuf.at[other], fbuf.at[other], f_ssem.at[d - 1], f_rsem.at[other], shift=other).wait_recv()
    for t in range(S):
        lo, hi = t * L, min(t * L + L, nl)
        if lo < hi:
            off = lo - min(lo, nl - L)
            for r in range(3):
                out_ref[r : r + 1, lo * LANE : hi * LANE] = fbuf[
                    t, r : r + 1, off * LANE : (off + hi - lo) * LANE
                ]

    for c in sh_copies:
        c.wait_send()
    for c in ag_pair(0, mate):
        c.wait_send()
    r1_copy(chip).wait_send()

    def drain(k, carry):
        for c in ag_pair(k, chip_at(k) * 2 + core):
            c.wait_send()
        for c in relay_pair(lax.rem(chip + NC - k, NC) * 2 + core):
            c.wait_send()
        r1_copy(chip_at(k)).wait_send()
        r2_copy(k).wait_send()
        return carry

    lax.fori_loop(1, NC, drain, 0)

    def drain_sc(b, carry):
        for d in range(1, S):
            sc_copy(b, d).wait_send()
        return carry

    lax.fori_loop(0, NB, drain_sc, 0)
    for d in range(1, S):
        f_copy(d).wait_send()


def local(W, S, particles, group_id, ctf_curves, projections, inv_noise, shifts):
    R = particles.shape[0]
    coeffs = inv_noise.shape[0]
    nl = coeffs // LANE
    L = -(-nl // S)
    C = L * LANE
    NTL = shifts.shape[0]
    NT = NTL * S
    H = W // 2
    NB = H // 2
    G = -(-W // LANE) * LANE
    rows = H * NT
    any_spec = pl.BlockSpec(memory_space=pl.ANY)
    vm = pl.BlockSpec(memory_space=pltpu.VMEM)
    dma = pltpu.SemaphoreType.DMA
    sh = jnp.pad(shifts.astype(F32), ((0, 0), (0, LANE - shifts.shape[1])))
    V = pltpu.VMEM
    out, ev = pl.pallas_call(
        functools.partial(kernel, (W, S, nl, L, NTL, R)),
        out_shape=(
            jax.ShapeDtypeStruct((3, coeffs), F32),
            jax.ShapeDtypeStruct((1, R), F32),
        ),
        in_specs=[any_spec, vm, vm, vm, vm, vm],
        out_specs=(vm, vm),
        scratch_shapes=[
            V((2, R, C), BF16),
            V((W, 1, C), F32),
            V((W, 2, C), BF16),
            V((S, NTL, LANE), F32),
            V((NT, C), F32),
            V((NT, C), F32),
            V((R, 2 * C), BF16),
            V((R, 2 * C), BF16),
            V((W, C), F32),
            V((W, 2, C), F32),
            V((W, C), F32),
            V((H, 2 * R), F32),
            V((rows, 2 * R), F32),
            V((max(S - 1, 1), rows, 2 * R), F32),
            V((rows, 2 * R), F32),
            V((2, rows, R), BF16),
            V((H, 2 * R), F32),
            V((W, 2, C + G), F32),
            V((W // 2, 2, C + G), F32),
            V((W // 2, 2, C + G), F32),
            V((2, C + G), F32),
            V((S, 4, C), F32),
            dma((2,)), dma((3,)),
            dma((2, W // 2)), dma((2, W)), dma((2, W)),
            dma((S,)), dma((S,)),
            dma((S, NB)), dma((S, NB)),
            dma((W // 2,)), dma((W // 2,)),
            dma((W // 2,)), dma((W // 2,)),
            dma((S,)), dma((S,)),
        ],
        compiler_params=pltpu.CompilerParams(
            collective_id=0, has_side_effects=True, vmem_limit_bytes=60 * 1024 * 1024
        ),
    )(
        particles, group_id, ctf_curves, projections.reshape(2, coeffs),
        inv_noise.reshape(1, coeffs), sh,
    )
    return out.reshape(1, 3 * coeffs), ev.reshape(R)


def solution(mesh):
    W, S = mesh.shape["wide"], mesh.shape["shift"]
    placed = (
        P("wide", None),
        P("wide", None),
        P("wide", None),
        P("wide", None),
        P(),
        P("shift", None),
    )
    return jax.shard_map(
        functools.partial(local, W, S), mesh=mesh, in_specs=placed,
        out_specs=(P("wide", None), P("wide")), check_vma=False,
    )
```

```python
import functools
import math

import jax
import jax.numpy as jnp
from jax import lax
from jax.experimental import pallas as pl
from jax.experimental.pallas import tpu as pltpu
from jax.sharding import PartitionSpec as P

LANE = 128
STEP = 2.0 * math.pi / 128.0
HIGH = lax.Precision.HIGHEST
MESH = pl.DeviceIdType.MESH
F32 = jnp.float32
BF16 = jnp.bfloat16
NT_DIMS = (((1,), (1,)), ((), ()))
NN_DIMS = (((1,), (0,)), ((), ()))
TN_DIMS = (((0,), (0,)), ((), ()))


def dot(a, b, dims=NN_DIMS, precision=None):
    return lax.dot_general(a, b, dims, precision=precision, preferred_element_type=F32)


def kernel(
    cfg, x_hbm, gid_ref, ctf_ref, proj_ref, noise_ref, sh_ref,
    out_ref, ev_ref,
    xbuf, cbuf, pbuf, shbuf, prow, nbuf, cos_t, sin_t, wgt, fil, wsq, pf, power, selfc,
    sc, scr, tot, wts, wsum, part, r1, r2, fin, fbuf,
    x_sem, own_sem, ag_ssem, ag_rsem, rl_ssem, sh_ssem, sh_rsem,
    sc_ssem, sc_rsem, r1_ssem, r1_rsem, r2_ssem, r2_rsem, f_ssem, f_rsem,
):
    W, S, nl, L, NTL, R = cfg
    C = L * LANE
    NT = NTL * S
    H = W // 2
    NC = W // 2
    QB = 2
    NB = H // QB
    RB = QB * NT
    w = lax.axis_index("wide")
    s = lax.axis_index("shift")
    core = lax.rem(w, 2)
    chip = lax.div(w, 2)
    mate = chip * 2 + (1 - core)
    first = jnp.minimum(s * L, nl - L)
    start = pl.multiple_of(first * LANE, LANE)
    full = nl * LANE
    window = pl.ds(start, C)

    def chip_at(k):
        return lax.rem(chip + k, NC)

    def remote(src, dst, ssem, rsem, wide=None, shift=None):
        return pltpu.make_async_remote_copy(
            src_ref=src, dst_ref=dst, send_sem=ssem, recv_sem=rsem,
            device_id=(w if wide is None else wide, s if shift is None else shift),
            device_id_type=MESH,
        )

    x_copies = [
        pltpu.make_async_copy(
            x_hbm.at[:, pl.ds(pl.multiple_of(start + h * full, LANE), C)],
            xbuf.at[h], x_sem.at[h],
        )
        for h in range(2)
    ]
    own = [
        pltpu.make_async_copy(ctf_ref.at[:, window], cbuf.at[w], own_sem.at[0]),
        pltpu.make_async_copy(proj_ref, prow, own_sem.at[1]),
        pltpu.make_async_copy(sh_ref, shbuf.at[s], own_sem.at[2]),
        pltpu.make_async_copy(noise_ref, nbuf.at[0], own_sem.at[3]),
    ]
    for c in own + x_copies:
        c.start()

    own[1].wait()
    for h in range(2):
        pbuf[w, h : h + 1, :] = prow[:, pl.ds(pl.multiple_of(start + h * full, LANE), C)]

    bar = pltpu.get_barrier_semaphore()
    pl.semaphore_signal(bar, inc=1, device_id=(mate, s), device_id_type=MESH)

    def greet(k, carry):
        pl.semaphore_signal(
            bar, inc=1, device_id=(chip_at(k) * 2 + core, s), device_id_type=MESH
        )
        return carry

    lax.fori_loop(1, NC, greet, 0)
    for d in range(1, S):
        pl.semaphore_signal(
            bar, inc=1, device_id=(w, lax.rem(s + d, S)), device_id_type=MESH
        )
    pl.semaphore_wait(bar, NC + S - 1)

    def ag_pair(k, to):
        return (
            remote(ctf_ref.at[:, window], cbuf.at[w], ag_ssem.at[0, k], ag_rsem.at[0, w], wide=to),
            remote(pbuf.at[w], pbuf.at[w], ag_ssem.at[1, k], ag_rsem.at[1, w], wide=to),
        )

    def relay_pair(src):
        return (
            remote(cbuf.at[src], cbuf.at[src], rl_ssem.at[0, src], ag_rsem.at[0, src], wide=mate),
            remote(pbuf.at[src], pbuf.at[src], rl_ssem.at[1, src], ag_rsem.at[1, src], wide=mate),
        )

    sh_copies = [
        remote(sh_ref, shbuf.at[s], sh_ssem.at[d - 1], sh_rsem.at[s], shift=lax.rem(s + d, S))
        for d in range(1, S)
    ]
    for c in sh_copies:
        c.start()

    def ag_start(k, carry):
        for c in ag_pair(k, chip_at(k) * 2 + core):
            c.start()
        return carry

    lax.fori_loop(1, NC, ag_start, 0)
    for c in ag_pair(0, mate):
        c.start()

    for c in own[:1] + own[2:]:
        c.wait()
    for d in range(1, S):
        other = lax.rem(s + d, S)
        remote(sh_ref, shbuf.at[other], sh_ssem.at[d - 1], sh_rsem.at[other], shift=other).wait_recv()

    lane = lax.broadcasted_iota(jnp.int32, (2, 2 * LANE), 1)
    axis = lax.broadcasted_iota(jnp.int32, (2, 2 * LANE), 0)
    freq = jnp.where(
        lane < LANE, jnp.where(axis == 0, first + lane, 0), jnp.where(axis == 1, lane - LANE - 64, 0)
    ).astype(F32)
    ang = STEP * jnp.concatenate(
        [dot(shbuf[t].astype(F32), freq, TN_DIMS, HIGH) for t in range(S)], axis=0
    )
    ang_a, ang_b = ang[:, :LANE], ang[:, LANE:]
    kx = first + lax.broadcasted_iota(jnp.int32, (NT, LANE), 1)
    live = jnp.where(kx >= s * L, 1.0, 0.0)
    cos_b, sin_b = jnp.cos(ang_b), jnp.sin(ang_b)
    cos_a, sin_a = jnp.cos(ang_a) * live, jnp.sin(ang_a) * live
    for l in range(L):
        ca, sa = cos_a[:, l : l + 1], sin_a[:, l : l + 1]
        cols = pl.ds(l * LANE, LANE)
        cos_t[:, cols] = ca * cos_b - sa * sin_b
        sin_t[:, cols] = sa * cos_b + ca * sin_b

    def relay(k, carry):
        src = lax.rem(chip + NC - k, NC) * 2 + core
        for c in relay_pair(src):
            c.wait_recv()
            c.start()
        return carry

    lax.fori_loop(1, NC, relay, 0)

    def landed(j, carry):
        for c in relay_pair(j * 2 + (1 - core)):
            c.wait_recv()
        return carry

    lax.fori_loop(0, NC, landed, 0)
    for c in x_copies:
        c.wait()

    onehot = jnp.where(
        gid_ref[...] == lax.broadcasted_iota(jnp.int32, (part.shape[2] - C, R), 0), 1.0, 0.0
    )
    pick = onehot[:W]
    for l in range(L):
        cols = pl.ds(l * LANE, LANE)
        curves = cbuf[:, 0, cols]
        row = dot(pick, curves, TN_DIMS, HIGH)
        noise = nbuf[:, pl.ds(pl.multiple_of(start + l * LANE, LANE), LANE)]
        x_re = xbuf[0, :, cols].astype(F32)
        x_im = xbuf[1, :, cols].astype(F32)
        gain = noise * row
        re, im = pl.ds(2 * l * LANE, LANE), pl.ds((2 * l + 1) * LANE, LANE)
        wgt[:, re] = (gain * x_re).astype(BF16)
        wgt[:, im] = (gain * x_im).astype(BF16)
        fil[:, re] = (row * x_re).astype(BF16)
        fil[:, im] = (row * x_im).astype(BF16)
        here = jnp.where(first + l >= s * L, 0.5, 0.0)
        wsq[:, cols] = curves * curves * noise * here

    def widen(o, carry):
        p = pbuf[o].astype(F32)
        pf[o] = p
        power[pl.ds(o, 1), :] = jnp.sum(p * p, axis=0, keepdims=True)
        return carry

    lax.fori_loop(0, W, widen, 0)
    self_g = dot(power[...], wsq[...], NT_DIMS, HIGH)
    self_i = dot(self_g, pick, NN_DIMS, HIGH)
    selfc[...] = jnp.concatenate([self_i[:H], self_i[H:]], axis=1)

    def sc_copy(b, d):
        rows = pl.ds(pl.multiple_of(b * RB, RB), RB)
        return remote(
            sc.at[rows], scr.at[d - 1, rows], sc_ssem.at[d - 1, b], sc_rsem.at[d - 1, b],
            shift=lax.rem(s + d, S),
        )

    def score_block(b, carry):
        acc = jnp.zeros((2 * RB, R), F32)
        for l in range(L):
            cols = pl.ds(l * LANE, LANE)
            ct, st = cos_t[:, cols], sin_t[:, cols]
            rots = []
            for h in range(2):
                for q in range(QB):
                    o = h * H + b * QB + q
                    pr = pf[o, 0:1, cols]
                    pi = pf[o, 1:2, cols]
                    rots.append(
                        jnp.concatenate(
                            [(pr * ct + pi * st).astype(BF16), (pi * ct - pr * st).astype(BF16)],
                            axis=1,
                        )
                    )
            rot = jnp.concatenate(rots, axis=0)
            acc = acc + dot(rot, wgt[:, pl.ds(2 * l * LANE, 2 * LANE)], NT_DIMS)
        both = jnp.concatenate([acc[:RB], acc[RB:]], axis=1)
        for q in range(QB):
            rows = pl.ds(pl.multiple_of(b * RB + q * NT, NT), NT)
            sc[rows, :] = both[q * NT : (q + 1) * NT] - selfc[pl.ds(b * QB + q, 1), :]
        for d in range(1, S):
            sc_copy(b, d).start()
        return carry

    lax.fori_loop(0, NB, score_block, 0)

    def swap(v):
        return pltpu.roll(v, R, 1)

    def join(b, m):
        rows = pl.ds(pl.multiple_of(b * RB, RB), RB)
        v = sc[rows, :]
        for d in range(1, S):
            sc_copy(b, d).wait_recv()
            v = v + scr[d - 1, rows, :]
        tot[rows, :] = v
        return jnp.maximum(m, jnp.max(v.reshape(RB // 8, 8, 2 * R), axis=0))

    m8 = lax.fori_loop(0, NB, join, jnp.full((8, 2 * R), -jnp.inf, F32))
    top = jnp.max(m8, axis=0, keepdims=True)
    top = jnp.maximum(top, swap(top))

    def expo(b, t):
        rows = pl.ds(pl.multiple_of(b * RB, RB), RB)
        e = jnp.exp(tot[rows, :] - top)
        tot[rows, :] = e
        return t + jnp.sum(e.reshape(RB // 8, 8, 2 * R), axis=0)

    t8 = lax.fori_loop(0, NB, expo, jnp.zeros((8, 2 * R), F32))
    total = jnp.sum(t8, axis=0, keepdims=True)
    total = total + swap(total)
    ev_ref[...] = (top + jnp.log(total))[:, :R]

    def norm(o, carry):
        rows = pl.ds(pl.multiple_of(o * NT, NT), NT)
        v = (tot[rows, :] / total).astype(BF16)
        wts[0, rows, :] = v[:, :R]
        wts[1, rows, :] = v[:, R:]
        wsum[pl.ds(o, 1), :] = jnp.sum(v.astype(F32), axis=0, keepdims=True)
        return carry

    lax.fori_loop(0, H, norm, 0)

    loads = wsum[...]
    extra = pl.ds(C, part.shape[2] - C)
    for h in range(2):
        load = dot(loads[:, h * R : (h + 1) * R], onehot, NT_DIMS, HIGH)
        for o in range(H):
            part[h * H + o, 0:1, extra] = load[o : o + 1]
            part[h * H + o, 1:2, extra] = jnp.zeros_like(load[o : o + 1])

    def r1_copy(j):
        return remote(part.at[2 * j + (1 - core)], r1.at[j], r1_ssem.at[j], r1_rsem.at[j], wide=mate)

    def r2_copy(k):
        to = chip_at(k)
        return remote(
            part.at[2 * to + core], r2.at[k], r2_ssem.at[k], r2_rsem.at[k], wide=2 * to + core
        )

    def update_chip(j):
        h = lax.div(2 * j, H)
        rows = pl.ds(pl.multiple_of(lax.rem(2 * j, H) * NT, 2 * NT), 2 * NT)
        pair = wts[h, rows, :]
        for l in range(L):
            cols = pl.ds(l * LANE, LANE)
            ct, st = cos_t[:, cols], sin_t[:, cols]
            u = dot(pair, fil[:, pl.ds(2 * l * LANE, 2 * LANE)])
            for q in range(2):
                ur = u[q * NT : (q + 1) * NT, :LANE]
                ui = u[q * NT : (q + 1) * NT, LANE:]
                part[2 * j + q, 0:1, cols] = jnp.sum(ur * ct - ui * st, axis=0, keepdims=True)
                part[2 * j + q, 1:2, cols] = jnp.sum(ur * st + ui * ct, axis=0, keepdims=True)

    def r1_take(k):
        j = chip_at(k)
        r1_copy(j).wait_recv()
        part[2 * j + core] = part[2 * j + core] + r1[j]
        r2_copy(k).start()

    def update_step(k, carry):
        j = chip_at(k)
        update_chip(j)
        r1_copy(j).start()

        @pl.when(jnp.logical_and(k >= 2, k <= NC))
        def _():
            r1_take(k - 1)

        return carry

    lax.fori_loop(1, NC + 1, update_step, 0)
    r1_copy(chip).wait_recv()
    fin[...] = part[w] + r1[chip]

    def r2_take(k, carry):
        r2_copy(k).wait_recv()
        fin[...] = fin[...] + r2[k]
        return carry

    lax.fori_loop(1, NC, r2_take, 0)

    load = fin[0:1, C : C + W]
    curves = cbuf[:, 0, :]
    fbuf[s, 0:2, :] = fin[:, :C]
    fbuf[s, 2:3, :] = dot(load, curves * curves, precision=HIGH)

    def f_copy(d):
        return remote(
            fbuf.at[s], fbuf.at[s], f_ssem.at[d - 1], f_rsem.at[s], shift=lax.rem(s + d, S)
        )

    for d in range(1, S):
        f_copy(d).start()
    for d in range(1, S):
        other = lax.rem(s + d, S)
        remote(fbuf.at[other], fbuf.at[other], f_ssem.at[d - 1], f_rsem.at[other], shift=other).wait_recv()
    for t in range(S):
        lo, hi = t * L, min(t * L + L, nl)
        if lo < hi:
            off = lo - min(lo, nl - L)
            for r in range(3):
                out_ref[r : r + 1, lo * LANE : hi * LANE] = fbuf[
                    t, r : r + 1, off * LANE : (off + hi - lo) * LANE
                ]

    for c in sh_copies:
        c.wait_send()
    for c in ag_pair(0, mate):
        c.wait_send()
    r1_copy(chip).wait_send()

    def drain(k, carry):
        for c in ag_pair(k, chip_at(k) * 2 + core):
            c.wait_send()
        for c in relay_pair(lax.rem(chip + NC - k, NC) * 2 + core):
            c.wait_send()
        r1_copy(chip_at(k)).wait_send()
        r2_copy(k).wait_send()
        return carry

    lax.fori_loop(1, NC, drain, 0)

    def drain_sc(b, carry):
        for d in range(1, S):
            sc_copy(b, d).wait_send()
        return carry

    lax.fori_loop(0, NB, drain_sc, 0)
    for d in range(1, S):
        f_copy(d).wait_send()


def unfold(rows_ref, ev_in, out_ref, ev_ref):
    n = rows_ref.shape[1]
    for r in range(3):
        out_ref[:, r * n : (r + 1) * n] = rows_ref[r : r + 1, :]
    ev_ref[...] = ev_in[...]


def local(W, S, particles, group_id, ctf_curves, projections, inv_noise, shifts):
    R = particles.shape[0]
    coeffs = inv_noise.shape[0]
    nl = coeffs // LANE
    L = -(-nl // S)
    C = L * LANE
    NTL = shifts.shape[0]
    NT = NTL * S
    H = W // 2
    NB = H // 2
    G = -(-W // LANE) * LANE
    rows = H * NT
    any_spec = pl.BlockSpec(memory_space=pl.ANY)
    vm = pl.BlockSpec(memory_space=pltpu.VMEM)
    dma = pltpu.SemaphoreType.DMA
    V = pltpu.VMEM
    out, ev = pl.pallas_call(
        functools.partial(kernel, (W, S, nl, L, NTL, R)),
        out_shape=(
            jax.ShapeDtypeStruct((3, coeffs), F32),
            jax.ShapeDtypeStruct((1, R), F32),
        ),
        in_specs=[any_spec, vm, any_spec, any_spec, any_spec, any_spec],
        out_specs=(vm, vm),
        scratch_shapes=[
            V((2, R, C), BF16),
            V((W, 1, C), F32),
            V((W, 2, C), BF16),
            V((S, 2, NTL), jnp.int32),
            V((1, 2 * coeffs), BF16),
            V((1, coeffs), F32),
            V((NT, C), F32),
            V((NT, C), F32),
            V((R, 2 * C), BF16),
            V((R, 2 * C), BF16),
            V((W, C), F32),
            V((W, 2, C), F32),
            V((W, C), F32),
            V((H, 2 * R), F32),
            V((rows, 2 * R), F32),
            V((max(S - 1, 1), rows, 2 * R), F32),
            V((rows, 2 * R), F32),
            V((2, rows, R), BF16),
            V((H, 2 * R), F32),
            V((W, 2, C + G), F32),
            V((W // 2, 2, C + G), F32),
            V((W // 2, 2, C + G), F32),
            V((2, C + G), F32),
            V((S, 4, C), F32),
            dma((2,)), dma((4,)),
            dma((2, W // 2)), dma((2, W)), dma((2, W)),
            dma((S,)), dma((S,)),
            dma((S, NB)), dma((S, NB)),
            dma((W // 2,)), dma((W // 2,)),
            dma((W // 2,)), dma((W // 2,)),
            dma((S,)), dma((S,)),
        ],
        compiler_params=pltpu.CompilerParams(
            collective_id=0, has_side_effects=True, vmem_limit_bytes=60 * 1024 * 1024
        ),
    )(
        particles, group_id.reshape(1, R), ctf_curves, projections, inv_noise, shifts.T,
    )
    out, ev = pl.pallas_call(
        unfold,
        out_shape=(
            jax.ShapeDtypeStruct((1, 3 * coeffs), F32),
            jax.ShapeDtypeStruct((1, R), F32),
        ),
        in_specs=[vm, vm],
        out_specs=(vm, vm),
    )(out, ev)
    return out, ev.reshape(R)


def solution(mesh):
    W, S = mesh.shape["wide"], mesh.shape["shift"]
    placed = (
        P("wide", None),
        P("wide", None),
        P("wide", None),
        P("wide", None),
        P(),
        P("shift", None),
    )
    return jax.shard_map(
        functools.partial(local, W, S), mesh=mesh, in_specs=placed,
        out_specs=(P("wide", None), P("wide")), check_vma=False,
    )
```

```python
import functools
import math

import jax
import jax.numpy as jnp
from jax import lax
from jax.experimental import pallas as pl
from jax.experimental.pallas import tpu as pltpu
from jax.sharding import PartitionSpec as P

LANE = 128
STEP = 2.0 * math.pi / 128.0
HIGH = lax.Precision.HIGHEST
MESH = pl.DeviceIdType.MESH
F32 = jnp.float32
BF16 = jnp.bfloat16
NT_DIMS = (((1,), (1,)), ((), ()))
NN_DIMS = (((1,), (0,)), ((), ()))
TN_DIMS = (((0,), (0,)), ((), ()))


def dot(a, b, dims=NN_DIMS, precision=None):
    return lax.dot_general(a, b, dims, precision=precision, preferred_element_type=F32)


def kernel(
    cfg, x_hbm, gid_ref, ctf_ref, proj_ref, noise_ref, sh_ref,
    out_ref, ev_ref,
    xbuf, cbuf, pbuf, shbuf, prow, nbuf, cos_t, sin_t, wgt, fil, wsq, pf, power, selfc, selfr, selft, rowbuf,
    sc, scr, tot, wts, wsum, part, r1, r2, fin, fbuf,
    x_sem, own_sem, ag_ssem, ag_rsem, rl_ssem, sh_ssem, sh_rsem,
    sc_ssem, sc_rsem, r1_ssem, r1_rsem, r2_ssem, r2_rsem, f_ssem, f_rsem,
):
    W, S, nl, L, NTL, R = cfg
    C = L * LANE
    NT = NTL * S
    H = W // 2
    NC = W // 2
    QB = 2
    NB = H // QB
    RB = QB * NT
    w = lax.axis_index("wide")
    s = lax.axis_index("shift")
    core = lax.rem(w, 2)
    chip = lax.div(w, 2)
    mate = chip * 2 + (1 - core)
    first = jnp.minimum(s * L, nl - L)
    start = pl.multiple_of(first * LANE, LANE)
    full = nl * LANE
    window = pl.ds(start, C)

    def chip_at(k):
        return lax.rem(chip + k, NC)

    def remote(src, dst, ssem, rsem, wide=None, shift=None):
        return pltpu.make_async_remote_copy(
            src_ref=src, dst_ref=dst, send_sem=ssem, recv_sem=rsem,
            device_id=(w if wide is None else wide, s if shift is None else shift),
            device_id_type=MESH,
        )

    x_copies = [
        pltpu.make_async_copy(
            x_hbm.at[:, pl.ds(pl.multiple_of(start + h * full, LANE), C)],
            xbuf.at[h], x_sem.at[h],
        )
        for h in range(2)
    ]
    own = [
        pltpu.make_async_copy(ctf_ref.at[:, window], cbuf.at[w], own_sem.at[0]),
        pltpu.make_async_copy(proj_ref, prow, own_sem.at[1]),
        pltpu.make_async_copy(sh_ref, shbuf.at[s], own_sem.at[2]),
        pltpu.make_async_copy(noise_ref, nbuf.at[0], own_sem.at[3]),
    ]
    for c in own + x_copies:
        c.start()

    bar = pltpu.get_barrier_semaphore()
    pl.semaphore_signal(bar, inc=1, device_id=(mate, s), device_id_type=MESH)

    def greet(k, carry):
        pl.semaphore_signal(
            bar, inc=1, device_id=(chip_at(k) * 2 + core, s), device_id_type=MESH
        )
        return carry

    lax.fori_loop(1, NC, greet, 0)
    for d in range(1, S):
        pl.semaphore_signal(
            bar, inc=1, device_id=(w, lax.rem(s + d, S)), device_id_type=MESH
        )
    own[1].wait()
    for h in range(2):
        pbuf[w, h : h + 1, :] = prow[:, pl.ds(pl.multiple_of(start + h * full, LANE), C)]

    pl.semaphore_wait(bar, NC + S - 1)

    def ag_pair(k, to):
        return (
            remote(ctf_ref.at[:, window], cbuf.at[w], ag_ssem.at[0, k], ag_rsem.at[0, w], wide=to),
            remote(pbuf.at[w], pbuf.at[w], ag_ssem.at[1, k], ag_rsem.at[1, w], wide=to),
        )

    def relay_pair(src):
        return (
            remote(cbuf.at[src], cbuf.at[src], rl_ssem.at[0, src], ag_rsem.at[0, src], wide=mate),
            remote(pbuf.at[src], pbuf.at[src], rl_ssem.at[1, src], ag_rsem.at[1, src], wide=mate),
        )

    sh_copies = [
        remote(sh_ref, shbuf.at[s], sh_ssem.at[d - 1], sh_rsem.at[s], shift=lax.rem(s + d, S))
        for d in range(1, S)
    ]
    for c in sh_copies:
        c.start()

    def ag_start(k, carry):
        for c in ag_pair(k, chip_at(k) * 2 + core):
            c.start()
        return carry

    lax.fori_loop(1, NC, ag_start, 0)
    for c in ag_pair(0, mate):
        c.start()

    for c in own[:1] + own[2:]:
        c.wait()
    for d in range(1, S):
        other = lax.rem(s + d, S)
        remote(sh_ref, shbuf.at[other], sh_ssem.at[d - 1], sh_rsem.at[other], shift=other).wait_recv()

    lane = lax.broadcasted_iota(jnp.int32, (2, 2 * LANE), 1)
    axis = lax.broadcasted_iota(jnp.int32, (2, 2 * LANE), 0)
    freq = jnp.where(
        lane < LANE, jnp.where(axis == 0, first + lane, 0), jnp.where(axis == 1, lane - LANE - 64, 0)
    ).astype(F32)
    ang = STEP * jnp.concatenate(
        [dot(shbuf[t].astype(F32), freq, TN_DIMS, HIGH) for t in range(S)], axis=0
    )
    ang_a, ang_b = ang[:, :LANE], ang[:, LANE:]
    kx = first + lax.broadcasted_iota(jnp.int32, (NT, LANE), 1)
    live = jnp.where(kx >= s * L, 1.0, 0.0)
    cos_b, sin_b = jnp.cos(ang_b), jnp.sin(ang_b)
    cos_a, sin_a = jnp.cos(ang_a) * live, jnp.sin(ang_a) * live
    for l in range(L):
        ca, sa = cos_a[:, l : l + 1], sin_a[:, l : l + 1]
        cols = pl.ds(l * LANE, LANE)
        cos_t[:, cols] = ca * cos_b - sa * sin_b
        sin_t[:, cols] = sa * cos_b + ca * sin_b

    def relay(k, carry):
        src = lax.rem(chip + NC - k, NC) * 2 + core
        for c in relay_pair(src):
            c.wait_recv()
            c.start()
        return carry

    lax.fori_loop(1, NC, relay, 0)

    def landed(j, carry):
        for c in relay_pair(j * 2 + (1 - core)):
            c.wait_recv()
        return carry

    lax.fori_loop(0, NC, landed, 0)
    for c in x_copies:
        c.wait()

    onehot = jnp.where(
        gid_ref[...] == lax.broadcasted_iota(jnp.int32, (part.shape[2] - C, R), 0), 1.0, 0.0
    )
    pick = onehot[:W]
    for l in range(L):
        cols = pl.ds(l * LANE, LANE)
        curves = cbuf[:, 0, cols]
        row = dot(pick, curves, TN_DIMS, HIGH)
        noise = nbuf[:, pl.ds(pl.multiple_of(start + l * LANE, LANE), LANE)]
        x_re = xbuf[0, :, cols].astype(F32)
        x_im = xbuf[1, :, cols].astype(F32)
        gain = noise * row
        re, im = pl.ds(2 * l * LANE, LANE), pl.ds((2 * l + 1) * LANE, LANE)
        wgt[:, re] = (gain * x_re).astype(BF16)
        wgt[:, im] = (gain * x_im).astype(BF16)
        rowbuf[:, cols] = row

    def widen(o, carry):
        p = pbuf[o].astype(F32)
        pf[o] = p
        return carry

    lax.fori_loop(0, W, widen, 0)
    def sc_copy(b, d):
        rows = pl.ds(pl.multiple_of(b * RB, RB), RB)
        return remote(
            sc.at[rows], scr.at[d - 1, rows], sc_ssem.at[d - 1, b], sc_rsem.at[d - 1, b],
            shift=lax.rem(s + d, S),
        )

    def score_block(b, carry):
        acc = jnp.zeros((2 * RB, R), F32)
        for l in range(L):
            cols = pl.ds(l * LANE, LANE)
            ct, st = cos_t[:, cols], sin_t[:, cols]
            rots = []
            for h in range(2):
                for q in range(QB):
                    o = h * H + b * QB + q
                    pr = pf[o, 0:1, cols]
                    pi = pf[o, 1:2, cols]
                    rots.append(
                        jnp.concatenate(
                            [(pr * ct + pi * st).astype(BF16), (pi * ct - pr * st).astype(BF16)],
                            axis=1,
                        )
                    )
            rot = jnp.concatenate(rots, axis=0)
            acc = acc + dot(rot, wgt[:, pl.ds(2 * l * LANE, 2 * LANE)], NT_DIMS)
        both = jnp.concatenate([acc[:RB], acc[RB:]], axis=1)
        sc[pl.ds(pl.multiple_of(b * RB, RB), RB), :] = both
        for d in range(1, S):
            sc_copy(b, d).start()
        return carry

    lax.fori_loop(0, NB, score_block, 0)

    def square(o, carry):
        p = pf[o]
        power[pl.ds(o, 1), :] = jnp.sum(p * p, axis=0, keepdims=True)
        return carry

    lax.fori_loop(0, W, square, 0)
    for l in range(L):
        cols = pl.ds(l * LANE, LANE)
        curves = cbuf[:, 0, cols]
        noise = nbuf[:, pl.ds(pl.multiple_of(start + l * LANE, LANE), LANE)]
        here = jnp.where(first + l >= s * L, 0.5, 0.0)
        wsq[:, cols] = curves * curves * noise * here
    self_g = dot(power[...], wsq[...], NT_DIMS, HIGH)
    self_i = dot(self_g, pick, NN_DIMS, HIGH)
    selfc[...] = jnp.concatenate([self_i[:H], self_i[H:]], axis=1)

    def self_copy(d):
        return remote(
            selfc, selfr.at[d - 1], sc_ssem.at[d - 1, NB], sc_rsem.at[d - 1, NB],
            shift=lax.rem(s + d, S),
        )

    for d in range(1, S):
        self_copy(d).start()
    for l in range(L):
        cols = pl.ds(l * LANE, LANE)
        row = rowbuf[:, cols]
        fil[:, pl.ds(2 * l * LANE, LANE)] = (row * xbuf[0, :, cols].astype(F32)).astype(BF16)
        fil[:, pl.ds((2 * l + 1) * LANE, LANE)] = (row * xbuf[1, :, cols].astype(F32)).astype(BF16)
    self_all = selfc[...]
    for d in range(1, S):
        self_copy(d).wait_recv()
        self_all = self_all + selfr[d - 1]
    selft[...] = self_all

    def swap(v):
        return pltpu.roll(v, R, 1)

    def join(b, m):
        rows = pl.ds(pl.multiple_of(b * RB, RB), RB)
        v = sc[rows, :]
        for d in range(1, S):
            sc_copy(b, d).wait_recv()
            v = v + scr[d - 1, rows, :]
        for q in range(QB):
            u = v[q * NT : (q + 1) * NT] - selft[pl.ds(b * QB + q, 1), :]
            tot[pl.ds(pl.multiple_of(b * RB + q * NT, NT), NT), :] = u
            m = jnp.maximum(m, jnp.max(u.reshape(NT // 8, 8, 2 * R), axis=0))
        return m

    m8 = lax.fori_loop(0, NB, join, jnp.full((8, 2 * R), -jnp.inf, F32))
    top = jnp.max(m8, axis=0, keepdims=True)
    top = jnp.maximum(top, swap(top))

    def expo(b, t):
        rows = pl.ds(pl.multiple_of(b * RB, RB), RB)
        e = jnp.exp(tot[rows, :] - top)
        tot[rows, :] = e
        return t + jnp.sum(e.reshape(RB // 8, 8, 2 * R), axis=0)

    t8 = lax.fori_loop(0, NB, expo, jnp.zeros((8, 2 * R), F32))
    total = jnp.sum(t8, axis=0, keepdims=True)
    total = total + swap(total)
    ev_ref[...] = (top + jnp.log(total))[:, :R]

    def norm(o, carry):
        rows = pl.ds(pl.multiple_of(o * NT, NT), NT)
        v = (tot[rows, :] / total).astype(BF16)
        wts[0, rows, :] = v[:, :R]
        wts[1, rows, :] = v[:, R:]
        wsum[pl.ds(o, 1), :] = jnp.sum(v.astype(F32), axis=0, keepdims=True)
        return carry

    lax.fori_loop(0, H, norm, 0)

    loads = wsum[...]
    extra = pl.ds(C, part.shape[2] - C)
    for h in range(2):
        load = dot(loads[:, h * R : (h + 1) * R], onehot, NT_DIMS, HIGH)
        for o in range(H):
            part[h * H + o, 0:1, extra] = load[o : o + 1]
            part[h * H + o, 1:2, extra] = jnp.zeros_like(load[o : o + 1])

    def r1_copy(j):
        return remote(part.at[2 * j + (1 - core)], r1.at[j], r1_ssem.at[j], r1_rsem.at[j], wide=mate)

    def r2_copy(k):
        to = chip_at(k)
        return remote(
            part.at[2 * to + core], r2.at[k], r2_ssem.at[k], r2_rsem.at[k], wide=2 * to + core
        )

    def update_chip(j):
        h = lax.div(2 * j, H)
        rows = pl.ds(pl.multiple_of(lax.rem(2 * j, H) * NT, 2 * NT), 2 * NT)
        pair = wts[h, rows, :]
        for l in range(L):
            cols = pl.ds(l * LANE, LANE)
            ct, st = cos_t[:, cols], sin_t[:, cols]
            u = dot(pair, fil[:, pl.ds(2 * l * LANE, 2 * LANE)])
            for q in range(2):
                ur = u[q * NT : (q + 1) * NT, :LANE]
                ui = u[q * NT : (q + 1) * NT, LANE:]
                part[2 * j + q, 0:1, cols] = jnp.sum(ur * ct - ui * st, axis=0, keepdims=True)
                part[2 * j + q, 1:2, cols] = jnp.sum(ur * st + ui * ct, axis=0, keepdims=True)

    def r1_take(k):
        j = chip_at(k)
        r1_copy(j).wait_recv()
        part[2 * j + core] = part[2 * j + core] + r1[j]
        r2_copy(k).start()

    def update_step(k, carry):
        j = chip_at(k)
        update_chip(j)
        r1_copy(j).start()

        @pl.when(jnp.logical_and(k >= 2, k <= NC))
        def _():
            r1_take(k - 1)

        return carry

    lax.fori_loop(1, NC + 1, update_step, 0)
    r1_copy(chip).wait_recv()
    fin[...] = part[w] + r1[chip]

    def r2_take(k, carry):
        r2_copy(k).wait_recv()
        fin[...] = fin[...] + r2[k]
        return carry

    lax.fori_loop(1, NC, r2_take, 0)

    load = fin[0:1, C : C + W]
    curves = cbuf[:, 0, :]
    fbuf[s, 0:2, :] = fin[:, :C]
    fbuf[s, 2:3, :] = dot(load, curves * curves, precision=HIGH)

    def f_copy(d):
        return remote(
            fbuf.at[s], fbuf.at[s], f_ssem.at[d - 1], f_rsem.at[s], shift=lax.rem(s + d, S)
        )

    for d in range(1, S):
        f_copy(d).start()
    for d in range(1, S):
        other = lax.rem(s + d, S)
        remote(fbuf.at[other], fbuf.at[other], f_ssem.at[d - 1], f_rsem.at[other], shift=other).wait_recv()
    for t in range(S):
        lo, hi = t * L, min(t * L + L, nl)
        if lo < hi:
            off = lo - min(lo, nl - L)
            for r in range(3):
                out_ref[r : r + 1, lo * LANE : hi * LANE] = fbuf[
                    t, r : r + 1, off * LANE : (off + hi - lo) * LANE
                ]

    for c in sh_copies:
        c.wait_send()
    for c in ag_pair(0, mate):
        c.wait_send()
    r1_copy(chip).wait_send()

    def drain(k, carry):
        for c in ag_pair(k, chip_at(k) * 2 + core):
            c.wait_send()
        for c in relay_pair(lax.rem(chip + NC - k, NC) * 2 + core):
            c.wait_send()
        r1_copy(chip_at(k)).wait_send()
        r2_copy(k).wait_send()
        return carry

    lax.fori_loop(1, NC, drain, 0)

    def drain_sc(b, carry):
        for d in range(1, S):
            sc_copy(b, d).wait_send()
        return carry

    lax.fori_loop(0, NB, drain_sc, 0)
    for d in range(1, S):
        f_copy(d).wait_send()
        self_copy(d).wait_send()


def unfold(rows_ref, ev_in, out_ref, ev_ref):
    n = rows_ref.shape[1]
    for r in range(3):
        out_ref[:, r * n : (r + 1) * n] = rows_ref[r : r + 1, :]
    ev_ref[...] = ev_in[...]


def local(W, S, particles, group_id, ctf_curves, projections, inv_noise, shifts):
    R = particles.shape[0]
    coeffs = inv_noise.shape[0]
    nl = coeffs // LANE
    L = -(-nl // S)
    C = L * LANE
    NTL = shifts.shape[0]
    NT = NTL * S
    H = W // 2
    NB = H // 2
    G = -(-W // LANE) * LANE
    rows = H * NT
    any_spec = pl.BlockSpec(memory_space=pl.ANY)
    vm = pl.BlockSpec(memory_space=pltpu.VMEM)
    dma = pltpu.SemaphoreType.DMA
    V = pltpu.VMEM
    out, ev = pl.pallas_call(
        functools.partial(kernel, (W, S, nl, L, NTL, R)),
        out_shape=(
            jax.ShapeDtypeStruct((3, coeffs), F32),
            jax.ShapeDtypeStruct((1, R), F32),
        ),
        in_specs=[any_spec, vm, any_spec, any_spec, any_spec, any_spec],
        out_specs=(vm, vm),
        scratch_shapes=[
            V((2, R, C), BF16),
            V((W, 1, C), F32),
            V((W, 2, C), BF16),
            V((S, 2, NTL), jnp.int32),
            V((1, 2 * coeffs), BF16),
            V((1, coeffs), F32),
            V((NT, C), F32),
            V((NT, C), F32),
            V((R, 2 * C), BF16),
            V((R, 2 * C), BF16),
            V((W, C), F32),
            V((W, 2, C), F32),
            V((W, C), F32),
            V((H, 2 * R), F32),
            V((max(S - 1, 1), H, 2 * R), F32),
            V((H, 2 * R), F32),
            V((R, C), F32),
            V((rows, 2 * R), F32),
            V((max(S - 1, 1), rows, 2 * R), F32),
            V((rows, 2 * R), F32),
            V((2, rows, R), BF16),
            V((H, 2 * R), F32),
            V((W, 2, C + G), F32),
            V((W // 2, 2, C + G), F32),
            V((W // 2, 2, C + G), F32),
            V((2, C + G), F32),
            V((S, 4, C), F32),
            dma((2,)), dma((4,)),
            dma((2, W // 2)), dma((2, W)), dma((2, W)),
            dma((S,)), dma((S,)),
            dma((S, NB + 1)), dma((S, NB + 1)),
            dma((W // 2,)), dma((W // 2,)),
            dma((W // 2,)), dma((W // 2,)),
            dma((S,)), dma((S,)),
        ],
        compiler_params=pltpu.CompilerParams(
            collective_id=0, has_side_effects=True, vmem_limit_bytes=60 * 1024 * 1024
        ),
    )(
        particles, group_id.reshape(1, R), ctf_curves, projections, inv_noise, shifts.T,
    )
    out, ev = pl.pallas_call(
        unfold,
        out_shape=(
            jax.ShapeDtypeStruct((1, 3 * coeffs), F32),
            jax.ShapeDtypeStruct((1, R), F32),
        ),
        in_specs=[vm, vm],
        out_specs=(vm, vm),
    )(out, ev)
    return out, ev.reshape(R)


def solution(mesh):
    W, S = mesh.shape["wide"], mesh.shape["shift"]
    placed = (
        P("wide", None),
        P("wide", None),
        P("wide", None),
        P("wide", None),
        P(),
        P("shift", None),
    )
    return jax.shard_map(
        functools.partial(local, W, S), mesh=mesh, in_specs=placed,
        out_specs=(P("wide", None), P("wide")), check_vma=False,
    )
```

```python
import functools
import math

import jax
import jax.numpy as jnp
from jax import lax
from jax.experimental import pallas as pl
from jax.experimental.pallas import tpu as pltpu
from jax.sharding import PartitionSpec as P

LANE = 128
STEP = 2.0 * math.pi / 128.0
HIGH = lax.Precision.HIGHEST
MESH = pl.DeviceIdType.MESH
F32 = jnp.float32
BF16 = jnp.bfloat16
NT_DIMS = (((1,), (1,)), ((), ()))
NN_DIMS = (((1,), (0,)), ((), ()))
TN_DIMS = (((0,), (0,)), ((), ()))


def dot(a, b, dims=NN_DIMS, precision=None):
    return lax.dot_general(a, b, dims, precision=precision, preferred_element_type=F32)


def kernel(
    cfg, x_hbm, gid_ref, ctf_ref, proj_ref, noise_ref, sh_ref,
    out_ref, ev_ref,
    xbuf, cbuf, pbuf, shbuf, prow, nbuf, cos_t, sin_t, wgt, fil, wsq, power, selfc, selfr, selft, rowbuf,
    sc, scr, tot, wts, wsum, part, r1, r2, fin, fbuf,
    x_sem, own_sem, ag_ssem, ag_rsem, rl_ssem, sh_ssem, sh_rsem,
    sc_ssem, sc_rsem, r1_ssem, r1_rsem, r2_ssem, r2_rsem, f_ssem, f_rsem,
):
    W, S, nl, L, NTL, R = cfg
    C = L * LANE
    NT = NTL * S
    H = W // 2
    NC = W // 2
    QB = 2
    NB = H // QB
    RB = QB * NT
    w = lax.axis_index("wide")
    s = lax.axis_index("shift")
    core = lax.rem(w, 2)
    chip = lax.div(w, 2)
    mate = chip * 2 + (1 - core)
    first = jnp.minimum(s * L, nl - L)
    start = pl.multiple_of(first * LANE, LANE)
    full = nl * LANE
    window = pl.ds(start, C)

    def chip_at(k):
        return lax.rem(chip + k, NC)

    def remote(src, dst, ssem, rsem, wide=None, shift=None):
        return pltpu.make_async_remote_copy(
            src_ref=src, dst_ref=dst, send_sem=ssem, recv_sem=rsem,
            device_id=(w if wide is None else wide, s if shift is None else shift),
            device_id_type=MESH,
        )

    x_copies = [
        pltpu.make_async_copy(
            x_hbm.at[:, pl.ds(pl.multiple_of(start + h * full, LANE), C)],
            xbuf.at[h], x_sem.at[h],
        )
        for h in range(2)
    ]
    own = [
        pltpu.make_async_copy(ctf_ref.at[:, window], cbuf.at[w], own_sem.at[0]),
        pltpu.make_async_copy(proj_ref, prow, own_sem.at[1]),
        pltpu.make_async_copy(sh_ref, shbuf.at[s], own_sem.at[2]),
        pltpu.make_async_copy(noise_ref, nbuf.at[0], own_sem.at[3]),
    ]
    for c in own + x_copies:
        c.start()

    bar = pltpu.get_barrier_semaphore()
    pl.semaphore_signal(bar, inc=1, device_id=(mate, s), device_id_type=MESH)

    def greet(k, carry):
        pl.semaphore_signal(
            bar, inc=1, device_id=(chip_at(k) * 2 + core, s), device_id_type=MESH
        )
        return carry

    lax.fori_loop(1, NC, greet, 0)
    for d in range(1, S):
        pl.semaphore_signal(
            bar, inc=1, device_id=(w, lax.rem(s + d, S)), device_id_type=MESH
        )
    own[1].wait()
    for h in range(2):
        pbuf[w, h : h + 1, :] = prow[:, pl.ds(pl.multiple_of(start + h * full, LANE), C)]

    pl.semaphore_wait(bar, NC + S - 1)

    def ag_pair(k, to):
        return (
            remote(ctf_ref.at[:, window], cbuf.at[w], ag_ssem.at[0, k], ag_rsem.at[0, w], wide=to),
            remote(pbuf.at[w], pbuf.at[w], ag_ssem.at[1, k], ag_rsem.at[1, w], wide=to),
        )

    def relay_pair(src):
        return (
            remote(cbuf.at[src], cbuf.at[src], rl_ssem.at[0, src], ag_rsem.at[0, src], wide=mate),
            remote(pbuf.at[src], pbuf.at[src], rl_ssem.at[1, src], ag_rsem.at[1, src], wide=mate),
        )

    sh_copies = [
        remote(sh_ref, shbuf.at[s], sh_ssem.at[d - 1], sh_rsem.at[s], shift=lax.rem(s + d, S))
        for d in range(1, S)
    ]
    for c in sh_copies:
        c.start()

    def ag_start(k, carry):
        for c in ag_pair(k, chip_at(k) * 2 + core):
            c.start()
        return carry

    lax.fori_loop(1, NC, ag_start, 0)
    for c in ag_pair(0, mate):
        c.start()

    for c in own[:1] + own[2:]:
        c.wait()
    for d in range(1, S):
        other = lax.rem(s + d, S)
        remote(sh_ref, shbuf.at[other], sh_ssem.at[d - 1], sh_rsem.at[other], shift=other).wait_recv()

    lane = lax.broadcasted_iota(jnp.int32, (2, 2 * LANE), 1)
    axis = lax.broadcasted_iota(jnp.int32, (2, 2 * LANE), 0)
    freq = jnp.where(
        lane < LANE, jnp.where(axis == 0, first + lane, 0), jnp.where(axis == 1, lane - LANE - 64, 0)
    ).astype(F32)
    ang = STEP * jnp.concatenate(
        [dot(shbuf[t].astype(F32), freq, TN_DIMS, HIGH) for t in range(S)], axis=0
    )
    ang_a, ang_b = ang[:, :LANE], ang[:, LANE:]
    kx = first + lax.broadcasted_iota(jnp.int32, (NT, LANE), 1)
    live = jnp.where(kx >= s * L, 1.0, 0.0)
    cos_b, sin_b = jnp.cos(ang_b), jnp.sin(ang_b)
    cos_a, sin_a = jnp.cos(ang_a) * live, jnp.sin(ang_a) * live
    for l in range(L):
        ca, sa = cos_a[:, l : l + 1], sin_a[:, l : l + 1]
        cols = pl.ds(l * LANE, LANE)
        cos_t[:, cols] = ca * cos_b - sa * sin_b
        sin_t[:, cols] = sa * cos_b + ca * sin_b

    def relay(k, carry):
        src = lax.rem(chip + NC - k, NC) * 2 + core
        for c in relay_pair(src):
            c.wait_recv()
            c.start()
        return carry

    lax.fori_loop(1, NC, relay, 0)

    def landed(j, carry):
        for c in relay_pair(j * 2 + (1 - core)):
            c.wait_recv()
        return carry

    lax.fori_loop(0, NC, landed, 0)
    for c in x_copies:
        c.wait()

    onehot = jnp.where(
        gid_ref[...] == lax.broadcasted_iota(jnp.int32, (part.shape[2] - C, R), 0), 1.0, 0.0
    )
    pick = onehot[:W]
    for l in range(L):
        cols = pl.ds(l * LANE, LANE)
        curves = cbuf[:, 0, cols]
        row = dot(pick, curves, TN_DIMS, HIGH)
        noise = nbuf[:, pl.ds(pl.multiple_of(start + l * LANE, LANE), LANE)]
        x_re = xbuf[0, :, cols].astype(F32)
        x_im = xbuf[1, :, cols].astype(F32)
        gain = noise * row
        re, im = pl.ds(2 * l * LANE, LANE), pl.ds((2 * l + 1) * LANE, LANE)
        wgt[:, re] = (gain * x_re).astype(BF16)
        wgt[:, im] = (gain * x_im).astype(BF16)
        rowbuf[:, cols] = row

    def sc_copy(b, d):
        rows = pl.ds(pl.multiple_of(b * RB, RB), RB)
        return remote(
            sc.at[rows], scr.at[d - 1, rows], sc_ssem.at[d - 1, b], sc_rsem.at[d - 1, b],
            shift=lax.rem(s + d, S),
        )

    def score_block(b, carry):
        acc = jnp.zeros((2 * RB, R), F32)
        for l in range(L):
            cols = pl.ds(l * LANE, LANE)
            ct, st = cos_t[:, cols], sin_t[:, cols]
            rots = []
            for h in range(2):
                for q in range(QB):
                    o = h * H + b * QB + q
                    pair = pbuf[o, :, cols].astype(F32)
                    pr, pi = pair[0:1], pair[1:2]
                    rots.append(
                        jnp.concatenate(
                            [(pr * ct + pi * st).astype(BF16), (pi * ct - pr * st).astype(BF16)],
                            axis=1,
                        )
                    )
            rot = jnp.concatenate(rots, axis=0)
            acc = acc + dot(rot, wgt[:, pl.ds(2 * l * LANE, 2 * LANE)], NT_DIMS)
        both = jnp.concatenate([acc[:RB], acc[RB:]], axis=1)
        sc[pl.ds(pl.multiple_of(b * RB, RB), RB), :] = both
        for d in range(1, S):
            sc_copy(b, d).start()
        return carry

    lax.fori_loop(0, NB, score_block, 0)

    def square(o, carry):
        p = pbuf[o].astype(F32)
        power[pl.ds(o, 1), :] = jnp.sum(p * p, axis=0, keepdims=True)
        return carry

    lax.fori_loop(0, W, square, 0)
    for l in range(L):
        cols = pl.ds(l * LANE, LANE)
        curves = cbuf[:, 0, cols]
        noise = nbuf[:, pl.ds(pl.multiple_of(start + l * LANE, LANE), LANE)]
        here = jnp.where(first + l >= s * L, 0.5, 0.0)
        wsq[:, cols] = curves * curves * noise * here
    self_g = dot(power[...], wsq[...], NT_DIMS, HIGH)
    self_i = dot(self_g, pick, NN_DIMS, HIGH)
    selfc[...] = jnp.concatenate([self_i[:H], self_i[H:]], axis=1)

    def self_copy(d):
        return remote(
            selfc, selfr.at[d - 1], sc_ssem.at[d - 1, NB], sc_rsem.at[d - 1, NB],
            shift=lax.rem(s + d, S),
        )

    for d in range(1, S):
        self_copy(d).start()
    for l in range(L):
        cols = pl.ds(l * LANE, LANE)
        row = rowbuf[:, cols]
        fil[:, pl.ds(2 * l * LANE, LANE)] = (row * xbuf[0, :, cols].astype(F32)).astype(BF16)
        fil[:, pl.ds((2 * l + 1) * LANE, LANE)] = (row * xbuf[1, :, cols].astype(F32)).astype(BF16)
    self_all = selfc[...]
    for d in range(1, S):
        self_copy(d).wait_recv()
        self_all = self_all + selfr[d - 1]
    selft[...] = self_all

    def swap(v):
        return pltpu.roll(v, R, 1)

    def join(b, m):
        rows = pl.ds(pl.multiple_of(b * RB, RB), RB)
        v = sc[rows, :]
        for d in range(1, S):
            sc_copy(b, d).wait_recv()
            v = v + scr[d - 1, rows, :]
        for q in range(QB):
            u = v[q * NT : (q + 1) * NT] - selft[pl.ds(b * QB + q, 1), :]
            tot[pl.ds(pl.multiple_of(b * RB + q * NT, NT), NT), :] = u
            m = jnp.maximum(m, jnp.max(u.reshape(NT // 8, 8, 2 * R), axis=0))
        return m

    m8 = lax.fori_loop(0, NB, join, jnp.full((8, 2 * R), -jnp.inf, F32))
    top = jnp.max(m8, axis=0, keepdims=True)
    top = jnp.maximum(top, swap(top))

    def expo(b, t):
        rows = pl.ds(pl.multiple_of(b * RB, RB), RB)
        e = jnp.exp(tot[rows, :] - top)
        tot[rows, :] = e
        return t + jnp.sum(e.reshape(RB // 8, 8, 2 * R), axis=0)

    t8 = lax.fori_loop(0, NB, expo, jnp.zeros((8, 2 * R), F32))
    total = jnp.sum(t8, axis=0, keepdims=True)
    total = total + swap(total)
    ev_ref[...] = (top + jnp.log(total))[:, :R]

    def norm(o, carry):
        rows = pl.ds(pl.multiple_of(o * NT, NT), NT)
        v = (tot[rows, :] / total).astype(BF16)
        wts[0, rows, :] = v[:, :R]
        wts[1, rows, :] = v[:, R:]
        wsum[pl.ds(o, 1), :] = jnp.sum(v.astype(F32), axis=0, keepdims=True)
        return carry

    lax.fori_loop(0, H, norm, 0)

    loads = wsum[...]
    extra = pl.ds(C, part.shape[2] - C)
    for h in range(2):
        load = dot(loads[:, h * R : (h + 1) * R], onehot, NT_DIMS, HIGH)
        for o in range(H):
            part[h * H + o, 0:1, extra] = load[o : o + 1]
            part[h * H + o, 1:2, extra] = jnp.zeros_like(load[o : o + 1])

    def r1_copy(j):
        return remote(part.at[2 * j + (1 - core)], r1.at[j], r1_ssem.at[j], r1_rsem.at[j], wide=mate)

    def r2_copy(k):
        to = chip_at(k)
        return remote(
            part.at[2 * to + core], r2.at[k], r2_ssem.at[k], r2_rsem.at[k], wide=2 * to + core
        )

    def update_chip(j):
        h = lax.div(2 * j, H)
        rows = pl.ds(pl.multiple_of(lax.rem(2 * j, H) * NT, 2 * NT), 2 * NT)
        pair = wts[h, rows, :]
        for l in range(L):
            cols = pl.ds(l * LANE, LANE)
            ct, st = cos_t[:, cols], sin_t[:, cols]
            u = dot(pair, fil[:, pl.ds(2 * l * LANE, 2 * LANE)])
            for q in range(2):
                ur = u[q * NT : (q + 1) * NT, :LANE]
                ui = u[q * NT : (q + 1) * NT, LANE:]
                part[2 * j + q, 0:1, cols] = jnp.sum(ur * ct - ui * st, axis=0, keepdims=True)
                part[2 * j + q, 1:2, cols] = jnp.sum(ur * st + ui * ct, axis=0, keepdims=True)

    def r1_take(k):
        j = chip_at(k)
        r1_copy(j).wait_recv()
        part[2 * j + core] = part[2 * j + core] + r1[j]
        r2_copy(k).start()

    def update_step(k, carry):
        j = chip_at(k)
        update_chip(j)
        r1_copy(j).start()

        @pl.when(jnp.logical_and(k >= 2, k <= NC))
        def _():
            r1_take(k - 1)

        return carry

    lax.fori_loop(1, NC + 1, update_step, 0)
    r1_copy(chip).wait_recv()
    fin[...] = part[w] + r1[chip]

    def r2_take(k, carry):
        r2_copy(k).wait_recv()
        fin[...] = fin[...] + r2[k]
        return carry

    lax.fori_loop(1, NC, r2_take, 0)

    load = fin[0:1, C : C + W]
    curves = cbuf[:, 0, :]
    fbuf[s, 0:2, :] = fin[:, :C]
    fbuf[s, 2:3, :] = dot(load, curves * curves, precision=HIGH)

    def f_copy(d):
        return remote(
            fbuf.at[s], fbuf.at[s], f_ssem.at[d - 1], f_rsem.at[s], shift=lax.rem(s + d, S)
        )

    for d in range(1, S):
        f_copy(d).start()
    for d in range(1, S):
        other = lax.rem(s + d, S)
        remote(fbuf.at[other], fbuf.at[other], f_ssem.at[d - 1], f_rsem.at[other], shift=other).wait_recv()
    for t in range(S):
        lo, hi = t * L, min(t * L + L, nl)
        if lo < hi:
            off = lo - min(lo, nl - L)
            for r in range(3):
                out_ref[r : r + 1, lo * LANE : hi * LANE] = fbuf[
                    t, r : r + 1, off * LANE : (off + hi - lo) * LANE
                ]

    for c in sh_copies:
        c.wait_send()
    for c in ag_pair(0, mate):
        c.wait_send()
    r1_copy(chip).wait_send()

    def drain(k, carry):
        for c in ag_pair(k, chip_at(k) * 2 + core):
            c.wait_send()
        for c in relay_pair(lax.rem(chip + NC - k, NC) * 2 + core):
            c.wait_send()
        r1_copy(chip_at(k)).wait_send()
        r2_copy(k).wait_send()
        return carry

    lax.fori_loop(1, NC, drain, 0)

    def drain_sc(b, carry):
        for d in range(1, S):
            sc_copy(b, d).wait_send()
        return carry

    lax.fori_loop(0, NB, drain_sc, 0)
    for d in range(1, S):
        f_copy(d).wait_send()
        self_copy(d).wait_send()


def unfold(rows_ref, ev_in, out_ref, ev_ref):
    n = rows_ref.shape[1]
    for r in range(3):
        out_ref[:, r * n : (r + 1) * n] = rows_ref[r : r + 1, :]
    ev_ref[...] = ev_in[...]


def local(W, S, particles, group_id, ctf_curves, projections, inv_noise, shifts):
    R = particles.shape[0]
    coeffs = inv_noise.shape[0]
    nl = coeffs // LANE
    L = -(-nl // S)
    C = L * LANE
    NTL = shifts.shape[0]
    NT = NTL * S
    H = W // 2
    NB = H // 2
    G = -(-W // LANE) * LANE
    rows = H * NT
    any_spec = pl.BlockSpec(memory_space=pl.ANY)
    vm = pl.BlockSpec(memory_space=pltpu.VMEM)
    dma = pltpu.SemaphoreType.DMA
    V = pltpu.VMEM
    out, ev = pl.pallas_call(
        functools.partial(kernel, (W, S, nl, L, NTL, R)),
        out_shape=(
            jax.ShapeDtypeStruct((3, coeffs), F32),
            jax.ShapeDtypeStruct((1, R), F32),
        ),
        in_specs=[any_spec, vm, any_spec, any_spec, any_spec, any_spec],
        out_specs=(vm, vm),
        scratch_shapes=[
            V((2, R, C), BF16),
            V((W, 1, C), F32),
            V((W, 2, C), BF16),
            V((S, 2, NTL), jnp.int32),
            V((1, 2 * coeffs), BF16),
            V((1, coeffs), F32),
            V((NT, C), F32),
            V((NT, C), F32),
            V((R, 2 * C), BF16),
            V((R, 2 * C), BF16),
            V((W, C), F32),
            V((W, C), F32),
            V((H, 2 * R), F32),
            V((max(S - 1, 1), H, 2 * R), F32),
            V((H, 2 * R), F32),
            V((R, C), F32),
            V((rows, 2 * R), F32),
            V((max(S - 1, 1), rows, 2 * R), F32),
            V((rows, 2 * R), F32),
            V((2, rows, R), BF16),
            V((H, 2 * R), F32),
            V((W, 2, C + G), F32),
            V((W // 2, 2, C + G), F32),
            V((W // 2, 2, C + G), F32),
            V((2, C + G), F32),
            V((S, 4, C), F32),
            dma((2,)), dma((4,)),
            dma((2, W // 2)), dma((2, W)), dma((2, W)),
            dma((S,)), dma((S,)),
            dma((S, NB + 1)), dma((S, NB + 1)),
            dma((W // 2,)), dma((W // 2,)),
            dma((W // 2,)), dma((W // 2,)),
            dma((S,)), dma((S,)),
        ],
        compiler_params=pltpu.CompilerParams(
            collective_id=0, has_side_effects=True, vmem_limit_bytes=60 * 1024 * 1024
        ),
    )(
        particles, group_id.reshape(1, R), ctf_curves, projections, inv_noise, shifts.T,
    )
    out, ev = pl.pallas_call(
        unfold,
        out_shape=(
            jax.ShapeDtypeStruct((1, 3 * coeffs), F32),
            jax.ShapeDtypeStruct((1, R), F32),
        ),
        in_specs=[vm, vm],
        out_specs=(vm, vm),
    )(out, ev)
    return out, ev.reshape(R)


def solution(mesh):
    W, S = mesh.shape["wide"], mesh.shape["shift"]
    placed = (
        P("wide", None),
        P("wide", None),
        P("wide", None),
        P("wide", None),
        P(),
        P("shift", None),
    )
    return jax.shard_map(
        functools.partial(local, W, S), mesh=mesh, in_specs=placed,
        out_specs=(P("wide", None), P("wide")), check_vma=False,
    )
```
